32 devices in a mesh: expert: 8 (over z, x), shard: 4 (over y, core).
Axes of the slice: x: 2, y: 2, z: 4, core: 2. Of those that a mesh axis runs over, the one named last changes fastest.
Arguments:
- tokens: bfloat16 [2, 2048, 2048], P(None, ('expert', 'shard')), may hold values from -6 to 6
- cotangent: bfloat16 [2, 2048, 2048], P(None, ('expert', 'shard')), may hold values from -3 to 3
- segments: int32 [2, 8, 256], P(None, 'expert'), may hold values from 0 to 3, never falling along the last dimension, each value on 1 to 128 neighbouring positions
- routes: int32 [2, 2048, 4], P(None, ('expert', 'shard')), may hold values from 0 to 7, all different within a row; in each aligned block of 64 rows (0 to 63, 64 to 127, ..., all dimensions but the last counted through in order) at most 48 rows name the same one
- gate_weight: float32 [2, 2048, 4], P(None, ('expert', 'shard')), may hold values from 0.1 to 0.6
- gain_attn: bfloat16 [2048], P(('expert', 'shard')), may hold values from 0.5 to 1.5
- w_qkv: bfloat16 [3, 2048, 2048], P(None, 'expert', 'shard'), may hold values from -0.125 to 0.125
- b_qkv: bfloat16 [3, 16, 128], P(None, 'shard', 'expert'), may hold values from -0.59765625 to 0.59765625
- w_out: bfloat16 [2048, 2048], P('shard', 'expert'), may hold values from -0.25 to 0.25
- gain_ffn: bfloat16 [2048], P(('expert', 'shard')), may hold values from 0.5 to 1.5
- w_sgu: bfloat16 [2, 2048, 5632], P(None, 'expert', 'shard'), may hold values from -0.125 to 0.125
- w_sd: bfloat16 [5632, 2048], P('shard', 'expert'), may hold values from -0.078125 to 0.078125
- shared_gate: bfloat16 [2048], P(('expert', 'shard')), may hold values from -0.125 to 0.125
- w_egu: bfloat16 [8, 2, 2048, 1408], P('expert', None, 'shard'), may hold values from -0.125 to 0.125
- w_ed: bfloat16 [8, 1408, 2048], P('expert', 'shard'), may hold values from -0.15625 to 0.15625
Outputs:
- mixed: float32 [2, 2048, 2048], P(None, ('expert', 'shard'))
- grad_tokens: float32 [2, 2048, 2048], P(None, ('expert', 'shard'))
- grad_gate_weight: float32 [2, 2048, 4], P(None, ('expert', 'shard'))
- grad_gain_attn: float32 [2048], P(('expert', 'shard'))
- grad_w_qkv: float32 [3, 2048, 2048], P(None, 'expert', 'shard')
- grad_b_qkv: float32 [3, 16, 128], P(None, 'shard', 'expert')
- grad_w_out: float32 [2048, 2048], P('shard', 'expert')
- grad_gain_ffn: float32 [2048], P(('expert', 'shard'))
- grad_w_sgu: float32 [2, 2048, 5632], P(None, 'expert', 'shard')
- grad_w_sd: float32 [5632, 2048], P('shard', 'expert')
- grad_shared_gate: float32 [2048], P(('expert', 'shard'))
- grad_w_egu: float32 [8, 2, 2048, 1408], P('expert', None, 'shard')
- grad_w_ed: float32 [8, 1408, 2048], P('expert', 'shard')
The draws below stay inside these ranges and needn't reach their ends.
Inputs may be any that keep to these rules, and one draw needn't show every extreme that they name: `routes`: in each micro-batch, the 64 tokens of one device name one expert at most 48 times over all their choices; a token's 4 experts differ. `segments`: documents never cross sequences; each has at most 128 tokens.
All inputs are finite; a program needn't handle non-finite values.
Results may differ from the reference program's by a relative error of at most 0.014.
Values may be sent and summed in bfloat16 or wider, within the bound.
A program may use at most 320 MiB of HBM per device.

```python
import math
import jax
import jax.numpy as jnp
import numpy as np
from jax import lax

D = 2048
HEADS = 16
HD = 128
FF = 1408
SFF = 5632
TOP = 4
TOK_MB = 64
MICRO = 2
DOCS = 4
EXPERTS = 8
SEQ_LEN = 256
TOKENS = 2048
CAP = 48
DOC_MAX = 128
N_EXPERT = 8
N_SHARD = 4


def steps_of(rng, shape, shards, least, largest):
    gain = 1.0
    for dim, blocks in shards:
        steps = jax.random.uniform(jax.random.fold_in(jax.random.fold_in(rng, 6), dim), (blocks,), jnp.float32, least / len(shards), largest / len(shards))
        gain = gain * jnp.repeat(jnp.exp(steps), shape[dim] // blocks).reshape((-1,) + (1,) * (len(shape) - 1 - dim))
    return gain


def length_profile(number_of, total, most, lean):
    weights = [(1 << 20) // math.isqrt(standing ** lean) + 1 for standing in range(2, number_of + 1)]
    surplus, counts = total - most - (number_of - 1), [1] * (number_of - 1)
    while surplus > 0:
        free = [i for i in range(number_of - 1) if counts[i] < most]
        whole, left = sum([weights[i] for i in free]), surplus
        for i in free:
            more = min(most - counts[i], max(1, left * weights[i] // whole), surplus)
            counts[i] = counts[i] + more
            surplus = surplus - more
    return np.array([most] + counts)


def ragged_sizes(stream_key, count, total, reach, skew):
    if count == 2:
        one = jax.random.randint(stream_key, (), max(1, total - reach), min(reach, total - 1) + 1)
        return jnp.stack([one, total - one])
    tallies = jnp.asarray(length_profile(count, total, reach, skew), jnp.int32)
    twos = (count - 1) // 2
    giver, receiver = tallies[1:1 + 2 * twos:2], tallies[2:2 + 2 * twos:2]
    slack = jnp.minimum(giver - 1, reach - receiver)
    passed = jax.random.randint(jax.random.fold_in(stream_key, 1), (twos,), 0, 1 << 20) % (slack + 1)
    tallies = tallies.at[1:1 + 2 * twos:2].set(giver - passed).at[2:2 + 2 * twos:2].set(receiver + passed)
    return tallies[jax.random.permutation(jax.random.fold_in(stream_key, 2), count)]


def deal_out(key, own, number, rows, number_of, top, bound, skew):
    ranking = jax.random.permutation(key, number_of)
    heavy_load, usual = portions_of(number_of, rows * top, bound, skew, True), portions_of(number_of, rows * top, bound, skew, False)
    places = jnp.arange(number_of)

    def named(lengths, offset_by):
        used = int((lengths > 0).sum())
        fixed = max(1, used // 4)
        shifted = fixed + (places - fixed + offset_by * (used - fixed)) % max(1, number_of - fixed)
        return jnp.zeros((number_of,), jnp.int32).at[ranking[jnp.where(places < fixed, places, shifted)]].set(jnp.asarray(lengths, jnp.int32))

    lengths = jnp.where(number % 4 == 0, named(heavy_load, number // 4), named(usual, number - number // 4 - 1))
    mixed = jax.random.permutation(jax.random.fold_in(own, 3), number_of)
    giver, sink = mixed[0:number_of // 2 * 2:2], mixed[1:number_of // 2 * 2:2]
    slack = jnp.minimum(lengths[giver] - 1, bound - lengths[sink]) // 2
    slack = jnp.where((giver == ranking[0]) | (sink == ranking[0]) | (lengths[sink] == 0), 0, jnp.maximum(slack, 0))
    shifted = jax.random.randint(jax.random.fold_in(own, 4), (number_of // 2,), 0, 1 << 20) % (slack + 1)
    lengths = lengths.at[giver].add(-shifted).at[sink].add(shifted)
    items = jnp.searchsorted(jnp.cumsum(lengths), jnp.arange(rows * top), side="right").astype(jnp.int32)
    grid = items.reshape(top, rows).T
    grid = grid[jax.random.permutation(jax.random.fold_in(own, 1), rows)]
    offset_by = jax.random.randint(jax.random.fold_in(own, 2), (rows, 1), 0, top)
    return jnp.take_along_axis(grid, (jnp.arange(top)[None, :] + offset_by) % top, axis=1)


def portions_of(count, total, most, skew, full):
    loads = [(1 << 20) // math.isqrt(rank ** skew) + 1 for rank in range(1, count + 1)]
    largest = most if full else min(most, max(-(-total // count), total * loads[0] // sum(loads)))
    least = 1 if total - largest >= count - 1 else 0
    given, surplus = [largest] + [least] * (count - 1), total - largest - least * (count - 1)
    while surplus > 0:
        candidates = [i for i in range(1, count) if given[i] < largest] or [i for i in range(1, count) if given[i] < most]
        mass, budget = sum([loads[i] for i in candidates]), surplus
        for i in candidates:
            extra = min(most - given[i], max(1, budget * loads[i] // mass), surplus)
            given[i] = given[i] + extra
            surplus = surplus - extra
    return np.array(given)


def normal_values(stream_key, dims, deviation, bound, cuts=(), kind=jnp.bfloat16):
    entries = deviation * jax.random.normal(stream_key, dims, jnp.float32)
    if cuts:
        entries = entries * steps_of(stream_key, dims, cuts, -0.22, 0.18)
    return jnp.clip(entries, -bound, bound).astype(kind)


def setup_inputs(seed: int = 0) -> dict:
    key_of = jax.random.split(jax.random.key(seed), 16)
    tokens = normal_values(key_of[0], (MICRO, TOKENS, D), 1.0, 6.0, ((1, 32),))
    cotangent = normal_values(key_of[1], (MICRO, TOKENS, D), 0.5, 3.0, ((1, 32),))
    segments = jax.vmap(lambda own: jnp.searchsorted(jnp.cumsum(ragged_sizes(own, DOCS, SEQ_LEN, DOC_MAX, 2)), jnp.arange(SEQ_LEN), side="right"))(jax.random.split(key_of[2], MICRO * N_EXPERT)).reshape((MICRO, N_EXPERT, SEQ_LEN)).astype(jnp.int32)
    routes_keys = jax.random.split(jax.random.fold_in(key_of[3], 1), MICRO * TOKENS // TOK_MB)
    routes_turns = jax.random.permutation(jax.random.fold_in(key_of[3], 3), MICRO * TOKENS // TOK_MB)
    routes = jax.vmap(lambda own, number: deal_out(jax.random.fold_in(key_of[3], 2), own, number, TOK_MB, EXPERTS, TOP, CAP, 2))(routes_keys, routes_turns).reshape((MICRO, TOKENS, TOP))
    gate_weight = jnp.clip(0.1 + 0.5 * jax.random.uniform(key_of[4], (MICRO, TOKENS, TOP), jnp.float32) ** steps_of(key_of[4], (MICRO, TOKENS, TOP), ((1, 32),), -0.2, 0.2), 0.1, 0.6)
    gain_attn = jnp.clip(1.0 + 0.1 * jax.random.normal(key_of[5], (D,), jnp.float32), 0.5, 1.5).astype(jnp.bfloat16)
    w_qkv = normal_values(key_of[6], (3, D, D), D ** -0.5, 0.125, ((1, 8), (2, 4)))
    b_qkv = normal_values(key_of[7], (3, HEADS, HD), 0.1, 0.59765625, ((1, 4), (2, 8)))
    w_out = normal_values(key_of[8], (D, D), (D // 4) ** -0.5, 0.25, ((0, 4), (1, 8)))
    gain_ffn = jnp.clip(1.0 + 0.1 * jax.random.normal(key_of[9], (D,), jnp.float32), 0.5, 1.5).astype(jnp.bfloat16)
    w_sgu = normal_values(key_of[10], (2, D, SFF), D ** -0.5, 0.125, ((1, 8), (2, 4)))
    w_sd = normal_values(key_of[11], (SFF, D), SFF ** -0.5, 0.078125, ((0, 4), (1, 8)))
    shared_gate = normal_values(key_of[12], (D,), D ** -0.5, 0.125, ((0, 32),))
    w_egu = normal_values(key_of[13], (EXPERTS, 2, D, FF), D ** -0.5, 0.125, ((0, 8), (2, 4)))
    w_ed = normal_values(key_of[14], (EXPERTS, FF, D), FF ** -0.5, 0.15625, ((0, 8), (1, 4)))
    return {"tokens": tokens, "cotangent": cotangent, "segments": segments, "routes": routes, "gate_weight": gate_weight, "gain_attn": gain_attn, "w_qkv": w_qkv, "b_qkv": b_qkv, "w_out": w_out, "gain_ffn": gain_ffn, "w_sgu": w_sgu, "w_sd": w_sd, "shared_gate": shared_gate, "w_egu": w_egu, "w_ed": w_ed}


EPSILON = 1e-06
ROPE_BASE = 1000000.0
HIGHEST = lax.Precision.HIGHEST

@jax.custom_vjp
def low(v):
    return lax.optimization_barrier(v.astype(jnp.bfloat16)).astype(jnp.float32)

@jax.custom_vjp
def low_back(v):
    return v

def low_keep(v):
    return (low(v), None)

def low_pass(kept, grad):
    return (grad,)

def back_keep(v):
    return (v, None)

def back_low(kept, grad):
    return (low(grad),)
low.defvjp(low_keep, low_pass)
low_back.defvjp(back_keep, back_low)

def rms_norm(rows, gain_vec):
    inv_scale = lax.rsqrt(lax.optimization_barrier(jnp.mean(rows * rows, axis=-1, keepdims=True)) + EPSILON)
    return rows * inv_scale * gain_vec

def rotate(tensor, cosine, sine):
    half_size = tensor.shape[-1] // 2
    first_half = tensor[..., :half_size]
    second_half = tensor[..., half_size:]
    return jnp.concatenate([first_half * cosine - second_half * sine, first_half * sine + second_half * cosine], axis=-1)

def attend(queries, key_rows, values, labels):
    length = queries.shape[0]
    scores = jnp.einsum('qhd,khd->hqk', queries, key_rows, precision=HIGHEST) * HD ** (-0.5)
    position = jnp.arange(length)
    allowed = (labels[:, None] == labels[None, :]) & (position[:, None] >= position[None, :])
    scores = low_back(jnp.where(allowed[None], scores, -1e+30))
    peak_val = lax.optimization_barrier(jnp.max(scores, axis=-1, keepdims=True))
    expo_vals = jnp.exp(scores - peak_val)
    probabilities = low(expo_vals / lax.optimization_barrier(jnp.sum(expo_vals, axis=-1, keepdims=True)))
    return jnp.einsum('hqk,khd->qhd', probabilities, values, precision=HIGHEST)

def per_sequence(packed):
    return jax.checkpoint(attend)(packed[0], packed[1], packed[2], packed[3])

def forward(tokens, gate_weight, gain_attn, w_qkv, b_qkv, w_out, gain_ffn, w_sgu, w_sd, shared_gate, w_egu, w_ed, segments, routes):
    rows = tokens.reshape(-1, D)
    row_count = rows.shape[0]
    normed = low(rms_norm(rows, gain_attn))
    projected = jnp.einsum('nd,ide->ine', normed, w_qkv, precision=HIGHEST) + b_qkv.reshape(3, 1, D)
    projected = low_back(projected)
    position = (jnp.arange(row_count) % SEQ_LEN).astype(jnp.float32)
    frequency = ROPE_BASE ** (-jnp.arange(HD // 2).astype(jnp.float32) * 2.0 / HD)
    angles = position[:, None, None] * frequency[None, None, :]
    cosine = jnp.cos(angles)
    sine = jnp.sin(angles)
    split_heads = projected.reshape(3, row_count, HEADS, HD)
    queries = low(rotate(split_heads[0], cosine, sine))
    key_rows = low(rotate(split_heads[1], cosine, sine))
    values = low(split_heads[2])
    sequences = row_count // SEQ_LEN
    seq_shape = (sequences, SEQ_LEN, HEADS, HD)
    context = lax.map(per_sequence, (queries.reshape(seq_shape), key_rows.reshape(seq_shape), values.reshape(seq_shape), segments.reshape(sequences, SEQ_LEN)))
    context = low_back(low(context.reshape(row_count, D)))
    attention = low_back(jnp.dot(context, w_out, precision=HIGHEST))
    hidden = rows + attention
    normed_two = low(rms_norm(hidden, gain_ffn))
    shared_in = low_back(jnp.einsum('nd,idf->inf', normed_two, w_sgu, precision=HIGHEST))
    shared_act = low(jax.nn.silu(shared_in[0]) * shared_in[1])
    shared_sum = low_back(jnp.dot(shared_act, w_sd, precision=HIGHEST))
    opening = jax.nn.sigmoid(jnp.dot(normed_two, shared_gate, precision=HIGHEST))
    flat_routes = routes.reshape(row_count, TOP)
    flat_gate = gate_weight.reshape(row_count, TOP)
    row_limit = MICRO * N_EXPERT * N_SHARD * CAP

    def one_expert(packed):
        expert_id, weights_gu, weights_down = packed
        chosen = flat_routes == expert_id
        routed = jnp.any(chosen, axis=-1)
        weight_sum = lax.optimization_barrier(jnp.sum(jnp.where(chosen, flat_gate, 0.0), axis=-1))
        picked = jnp.nonzero(routed, size=row_limit, fill_value=0)[0].astype(jnp.int32)
        live_rows = (jnp.arange(row_limit) < jnp.sum(routed.astype(jnp.int32))).astype(jnp.float32)
        inputs = low_back(jnp.take(normed_two, picked, axis=0))
        gate_up = low_back(jnp.einsum('rd,idf->irf', inputs, weights_gu, precision=HIGHEST))
        activated = low(jax.nn.silu(gate_up[0]) * gate_up[1])
        result = low_back(low(jnp.dot(activated, weights_down, precision=HIGHEST)))
        return (result * (jnp.take(weight_sum, picked) * live_rows)[:, None], picked)
    outputs, picked_all = lax.map(jax.checkpoint(one_expert), (jnp.arange(EXPERTS).astype(jnp.int32), w_egu, w_ed))
    expert_mix = jnp.zeros((row_count, D), jnp.float32).at[picked_all.reshape(-1)].add(outputs.reshape(-1, D))
    mixed = hidden + opening[:, None] * shared_sum + expert_mix
    return mixed.reshape(tokens.shape)

def reference(tokens, cotangent, segments, routes, gate_weight, gain_attn, w_qkv, b_qkv, w_out, gain_ffn, w_sgu, w_sd, shared_gate, w_egu, w_ed):
    floats = (tokens.astype(jnp.float32), gate_weight.astype(jnp.float32), gain_attn.astype(jnp.float32), w_qkv.astype(jnp.float32), b_qkv.astype(jnp.float32), w_out.astype(jnp.float32), gain_ffn.astype(jnp.float32), w_sgu.astype(jnp.float32), w_sd.astype(jnp.float32), shared_gate.astype(jnp.float32), w_egu.astype(jnp.float32), w_ed.astype(jnp.float32))

    def closed(*arrays):
        return forward(*arrays, segments, routes)
    mixed, pullback = jax.vjp(closed, *floats)
    gradients = pullback(cotangent.astype(jnp.float32))
    return (mixed, gradients[0], gradients[1], gradients[2], gradients[3], gradients[4], gradients[5], gradients[6], gradients[7], gradients[8], gradients[9], gradients[10], gradients[11])
```

```python
import jax
import jax.numpy as jnp
from jax import lax
from jax.sharding import PartitionSpec as P

HD = 128
EPSILON = 1e-06
ROPE_BASE = 1000000.0
F32 = jnp.float32
BF16 = jnp.bfloat16


def dot(spec, left, right):
    return jnp.einsum(spec, left, right, preferred_element_type=F32)


def spread_rows(rows):
    return lax.all_gather(rows, "shard", axis=0, tiled=True)


def fold_rows(rows):
    return lax.psum_scatter(rows.astype(BF16), "shard", scatter_dimension=0, tiled=True).astype(F32)


def spread_experts(rows):
    return lax.all_gather(rows, "expert", axis=0, tiled=True)


def fold_experts(rows):
    return lax.psum_scatter(rows.astype(BF16), "expert", scatter_dimension=0, tiled=True).astype(F32)


def rotate(tensor, cosine, sine):
    half = tensor.shape[-1] // 2
    first, second = tensor[..., :half], tensor[..., half:]
    return jnp.concatenate([first * cosine - second * sine, first * sine + second * cosine], axis=-1)


def norm_back(grad_normed, source, inv_scale, gain):
    unit = source * inv_scale
    grad_unit = grad_normed * gain
    grad_source = inv_scale * (grad_unit - unit * jnp.mean(grad_unit * unit, axis=-1, keepdims=True))
    return grad_source, jnp.sum(grad_normed * unit, axis=0)


def swish_back(gate, up, grad_act):
    sig = jax.nn.sigmoid(gate)
    grad_gate = grad_act * up * sig * (1.0 + gate * (1.0 - sig))
    grad_up = grad_act * gate * sig
    return jnp.stack([grad_gate, grad_up]).astype(BF16)


def body(
    tokens, cotangent, segments, routes, gate_weight, gain_attn, w_qkv, b_qkv, w_out,
    gain_ffn, w_sgu, w_sd, shared_gate, w_egu, w_ed,
):
    micro, span, width = tokens.shape
    shards = lax.axis_size("shard")
    experts = lax.axis_size("expert") * w_egu.shape[0]
    own = w_egu.shape[0]
    count = micro * span
    length = span * shards
    heads = b_qkv.shape[1]
    score_scale = HD ** (-0.5)

    vectors = jnp.stack([gain_attn, gain_ffn, shared_gate])
    vectors = lax.all_gather(vectors, ("expert", "shard"), axis=1, tiled=True)
    bias = lax.all_gather(b_qkv, "expert", axis=2, tiled=True)
    qkv = lax.all_gather(w_qkv, "expert", axis=1, tiled=True)
    out = lax.all_gather(w_out, "expert", axis=1, tiled=True)
    sgu = lax.all_gather(w_sgu, "expert", axis=1, tiled=True)
    sd = lax.all_gather(w_sd, "expert", axis=1, tiled=True)
    egu = lax.all_gather(w_egu, "shard", axis=2, tiled=True)
    ed = lax.all_gather(w_ed, "shard", axis=1, tiled=True)

    gain_one, gain_two, gate_vec = (vectors[i].astype(F32) for i in range(3))
    source = tokens.reshape(count, width).astype(F32)
    grad_low = cotangent.reshape(count, width)
    grad_out = grad_low.astype(F32)
    chosen = (routes.reshape(count, -1)[:, :, None] == jnp.arange(experts)).astype(F32)
    gates = jnp.sum(chosen * gate_weight.reshape(count, -1)[:, :, None], axis=1)
    gates = gates.T.reshape(-1, own, count)
    gates = lax.all_to_all(gates, "expert", split_axis=0, concat_axis=0, tiled=True)
    gates = gates.transpose(1, 0, 2).reshape(own, -1)
    grad_all = spread_experts(grad_low)

    scale_one = lax.rsqrt(jnp.mean(source * source, axis=-1, keepdims=True) + EPSILON)
    normed_one = (source * scale_one * gain_one).astype(BF16)
    rows_one = spread_rows(normed_one)
    projected = dot("ld,ide->ile", rows_one, qkv) + bias.reshape(3, 1, -1).astype(F32)

    place = jnp.arange(length).astype(F32)
    frequency = ROPE_BASE ** (-jnp.arange(HD // 2).astype(F32) * 2.0 / HD)
    angles = place[:, None] * frequency[None, :]
    cosine, sine = jnp.cos(angles), jnp.sin(angles)

    def to_heads(rows):
        grid = rows.reshape(shards, micro, span, heads, HD).transpose(1, 3, 0, 2, 4)
        return grid.reshape(micro, heads, length, HD)

    def to_rows(grid):
        grid = grid.reshape(micro, heads, shards, span, HD).transpose(2, 0, 3, 1, 4)
        return grid.reshape(shards * count, heads * HD)

    queries = rotate(to_heads(projected[0]), cosine, sine).astype(BF16)
    keys = rotate(to_heads(projected[1]), cosine, sine).astype(BF16)
    values = to_heads(projected[2]).astype(BF16)
    labels = segments[:, 0]
    index = jnp.arange(length)
    allowed = (labels[:, :, None] == labels[:, None, :]) & (index[:, None] >= index[None, :])
    allowed = allowed[:, None]
    scores = jnp.where(allowed, dot("mhqd,mhkd->mhqk", queries, keys) * score_scale, -1e30)
    peak = jnp.max(scores, axis=-1, keepdims=True)
    expo = jnp.exp(scores - peak)
    total = jnp.sum(expo, axis=-1, keepdims=True)
    exact = expo / total
    probs = exact.astype(BF16)
    context = to_rows(dot("mhqk,mhkd->mhqd", probs, values).astype(BF16))
    hidden = source + fold_rows(dot("le,ed->ld", context, out))

    scale_two = lax.rsqrt(jnp.mean(hidden * hidden, axis=-1, keepdims=True) + EPSILON)
    normed_two = (hidden * scale_two * gain_two).astype(BF16)
    rows_two = spread_rows(normed_two)
    routed = spread_experts(normed_two)
    shared_in = dot("ld,idf->ilf", rows_two, sgu)
    shared_act = (jax.nn.silu(shared_in[0]) * shared_in[1]).astype(BF16)
    shared_sum = fold_rows(dot("lf,fd->ld", shared_act, sd))
    normed_float = normed_two.astype(F32)
    opening = jax.nn.sigmoid(jnp.sum(normed_float * gate_vec, axis=-1))

    expert_in = dot("rd,jidf->ijrf", routed, egu)
    expert_act = (jax.nn.silu(expert_in[0]) * expert_in[1]).astype(BF16)
    expert_out = dot("jrf,jfd->jrd", expert_act, ed).astype(BF16).astype(F32)
    blend = fold_experts(jnp.sum(gates[:, :, None] * expert_out, axis=0))
    mixed = hidden + opening[:, None] * shared_sum + blend
    grad_all_float = grad_all.astype(F32)
    inner = jnp.sum(expert_out * grad_all_float, axis=-1)
    inner = inner.reshape(own, -1, count).transpose(1, 0, 2)
    inner = lax.all_to_all(inner, "expert", split_axis=0, concat_axis=0, tiled=True)
    inner = inner.reshape(experts, count)
    grad_gate = jnp.sum(chosen * inner.T[:, None, :], axis=-1)

    grad_expert = (gates[:, :, None] * grad_all_float).astype(BF16)
    grad_expert_act = dot("jrd,jfd->jrf", grad_expert, ed)
    grad_ed = dot("jrf,jrd->jfd", expert_act, grad_expert)
    grad_expert_in = swish_back(expert_in[0], expert_in[1], grad_expert_act)
    grad_routed = dot("ijrf,jidf->rd", grad_expert_in, egu)
    grad_egu = dot("rd,ijrf->jidf", routed, grad_expert_in)
    grad_from_experts = fold_experts(grad_routed)

    grad_shared = (opening[:, None] * grad_out).astype(BF16)
    grad_shared_rows = spread_rows(grad_shared)
    grad_shared_act = dot("ld,fd->lf", grad_shared_rows, sd)
    grad_sd = dot("lf,ld->fd", shared_act, grad_shared_rows)
    grad_shared_in = swish_back(shared_in[0], shared_in[1], grad_shared_act)
    grad_sgu = dot("ld,ilf->idf", rows_two, grad_shared_in)
    grad_from_shared = fold_rows(dot("ilf,idf->ld", grad_shared_in, sgu))
    grad_opening = jnp.sum(grad_out * shared_sum, axis=-1)
    grad_logit = grad_opening * opening * (1.0 - opening)
    grad_gate_vec = jnp.sum(grad_logit[:, None] * normed_float, axis=0)
    grad_normed_two = grad_from_experts + grad_from_shared + grad_logit[:, None] * gate_vec
    grad_hidden, grad_gain_two = norm_back(grad_normed_two, hidden, scale_two, gain_two)
    grad_hidden = grad_out + grad_hidden

    grad_rows = spread_rows(grad_hidden.astype(BF16))
    grad_context = to_heads(dot("ld,ed->le", grad_rows, out).astype(BF16))
    grad_out_w = dot("le,ld->ed", context, grad_rows)
    grad_probs = dot("mhqd,mhkd->mhqk", grad_context, values)
    delta = jnp.sum(exact * grad_probs, axis=-1, keepdims=True)
    grad_scores = (exact * (grad_probs - delta)).astype(BF16)
    grad_values = dot("mhqk,mhqd->mhkd", probs, grad_context)
    grad_queries = dot("mhqk,mhkd->mhqd", grad_scores, keys) * score_scale
    grad_keys = dot("mhqk,mhqd->mhkd", grad_scores, queries) * score_scale
    grad_projected = jnp.stack(
        [
            to_rows(rotate(grad_queries, cosine, -sine)),
            to_rows(rotate(grad_keys, cosine, -sine)),
            to_rows(grad_values),
        ]
    ).astype(BF16)
    grad_bias = jnp.sum(grad_projected.astype(F32), axis=1).reshape(3, heads, HD)
    grad_qkv = dot("ld,ile->ide", rows_one, grad_projected)
    grad_normed_one = fold_rows(dot("ile,ide->ld", grad_projected, qkv))
    grad_source, grad_gain_one = norm_back(grad_normed_one, source, scale_one, gain_one)
    grad_tokens = grad_hidden + grad_source

    def fold_weights(value, axis, dim):
        return lax.psum_scatter(value.astype(BF16), axis, scatter_dimension=dim, tiled=True).astype(F32)

    summed_ed = fold_weights(grad_ed, "shard", 1)
    summed_egu = fold_weights(grad_egu, "shard", 2)
    summed_sd = fold_weights(grad_sd, "expert", 1)
    summed_sgu = fold_weights(grad_sgu, "expert", 1)
    summed_out = fold_weights(grad_out_w, "expert", 1)
    summed_qkv = fold_weights(grad_qkv, "expert", 1)
    summed_bias = lax.psum_scatter(grad_bias, "expert", scatter_dimension=2, tiled=True)
    gains = jnp.stack([grad_gain_one, grad_gain_two, grad_gate_vec])
    gains = lax.psum_scatter(gains, ("expert", "shard"), scatter_dimension=1, tiled=True)
    shape = tokens.shape
    return (
        mixed.reshape(shape),
        grad_tokens.reshape(shape),
        grad_gate.reshape(routes.shape),
        gains[0],
        summed_qkv,
        summed_bias,
        summed_out,
        gains[1],
        summed_sgu,
        summed_sd,
        gains[2],
        summed_egu,
        summed_ed,
    )


def solution(mesh):
    both = ("expert", "shard")
    rows = P(None, both, None)
    parameters = (
        P(None, "expert", "shard"),
        P(None, "shard", "expert"),
        P("shard", "expert"),
        P(both),
        P(None, "expert", "shard"),
        P("shard", "expert"),
        P(both),
        P("expert", None, "shard", None),
        P("expert", "shard", None),
    )
    return jax.shard_map(
        body,
        mesh=mesh,
        in_specs=(rows, rows, P(None, "expert", None), rows, rows, P(both)) + parameters,
        out_specs=(rows, rows, rows, P(both)) + parameters,
        check_vma=False,
    )
```

```python
import functools
import itertools

import jax
import jax.numpy as jnp
from jax import lax
from jax.experimental import pallas as pl
from jax.experimental.pallas import tpu as pltpu
from jax.sharding import PartitionSpec as P

HD = 128
EPSILON = 1e-06
ROPE_BASE = 1000000.0
F32 = jnp.float32
BF16 = jnp.bfloat16
MESH = pl.DeviceIdType.MESH
VMEM_BYTES = 62 * 1024 * 1024


def part(ref, dim, index, size):
    start = index * size
    if size % 128 == 0:
        start = pl.multiple_of(start, 128)
    elif size % 8 == 0:
        start = pl.multiple_of(start, 8)
    return ref.at[tuple(pl.ds(start, size) if i == dim else slice(None) for i in range(len(ref.shape)))]


def greet(sizes):
    barrier = pltpu.get_barrier_semaphore()
    total = 0
    for axis, size in sizes.items():
        me = lax.axis_index(axis)
        half, side, place = size // 2, me % 2, me // 2
        for step in range(1, half):
            peer = (place + step) % half * 2 + side
            pl.semaphore_signal(barrier, inc=1, device_id={axis: peer}, device_id_type=MESH)
        pl.semaphore_signal(barrier, inc=1, device_id={axis: me + 1 - 2 * side}, device_id_type=MESH)
        total += half
    pl.semaphore_wait(barrier, total)


def gather_kernel(plan, sizes, *refs):
    count = len(plan)
    ins, outs, stage = refs[:count], refs[count : 2 * count], refs[2 * count : 3 * count]
    send_sem, recv_sem, near_sem = refs[3 * count :]
    greet(sizes)
    base, slot = [0], [0]
    for axis, dim, first in plan:
        base.append(base[-1] + sizes[axis])
        slot.append(slot[-1] + 3 * sizes[axis])
    loads = []
    for i in range(count):
        load = pltpu.make_async_copy(ins[i], stage[i], near_sem.at[i, 0])
        load.start()
        loads.append(load)
    waits = []

    def copy_of(i, src, piece, device, number):
        axis, dim, first = plan[i]
        return pltpu.make_async_remote_copy(
            src_ref=src,
            dst_ref=part(outs[i], dim, piece, ins[i].shape[dim]),
            send_sem=send_sem.at[slot[i] + number],
            recv_sem=recv_sem.at[base[i] + piece],
            device_id={axis: device},
            device_id_type=MESH,
        )

    def push(i, src, piece, device, number, when=None):
        if when is None:
            copy_of(i, src, piece, device, number).start()
        else:
            pl.when(when)(lambda: copy_of(i, src, piece, device, number).start())
        waits.append((i, src, piece, device, number, when))

    def arrive(i, piece):
        axis, dim, first = plan[i]
        view = part(outs[i], dim, piece, ins[i].shape[dim])
        copy_of(i, view, piece, lax.axis_index(axis), 0).wait_recv()
        return view

    def where(i):
        axis = plan[i][0]
        me = lax.axis_index(axis)
        return me, sizes[axis] // 2, me % 2, me // 2

    def chain(i, src, piece, number, left, right):
        me, half, side, place = where(i)
        if right is not False:
            push(i, src, piece, me + 2, number, place < half - 1 if right is True else right)
        if left is not False:
            push(i, src, piece, me - 2, number + 1, place > 0 if left is True else left)

    for i, (axis, dim, first) in enumerate(plan):
        me, half, side, place = where(i)
        push(i, ins[i], me, me + 1 - 2 * side, 0)
        if half > 1:
            chain(i, ins[i], me, 1, True, True)
    stores = []
    for i, (axis, dim, first) in enumerate(plan):
        loads[i].wait()
        store = pltpu.make_async_copy(
            stage[i], part(outs[i], dim, lax.axis_index(axis), ins[i].shape[dim]), near_sem.at[i, 1]
        )
        store.start()
        stores.append(store)
    for i, (axis, dim, first) in enumerate(plan):
        me, half, side, place = where(i)
        mate = me + 1 - 2 * side
        number = 3
        if first:
            view = arrive(i, mate)
            chain(i, view, mate, number, True, True)
            number += 2
        for step in range(1, half):
            for turn in (-1, 1):
                ok = place >= step if turn < 0 else place < half - step
                on = (ok & (place < half - 1)) if turn < 0 else (ok & (place > 0))
                for flip in (False, True) if first else (False,):
                    piece = (mate if flip else me) + 2 * turn * step

                    @pl.when(ok)
                    def _(i=i, piece=piece):
                        arrive(i, piece)

                    view = part(outs[i], dim, piece, ins[i].shape[dim])
                    if step < half - 1:
                        push(i, view, piece, me - 2 * turn, number, on)
                        number += 1
                    if not first:
                        push(i, view, piece, mate, number, ok)
                        number += 1
    for i, (axis, dim, first) in enumerate(plan):
        me, half, side, place = where(i)
        if not first:
            for step in range(half):
                arrive(i, (place + step) % half * 2 + 1 - side)
    for i, src, piece, device, number, when in waits:
        if when is None:
            copy_of(i, src, piece, device, number).wait_send()
        else:
            pl.when(when)(lambda: copy_of(i, src, piece, device, number).wait_send())
    for store in stores:
        store.wait()


def aligned(size, array, dim):
    return size % (128 if dim == array.ndim - 1 else 16) == 0


def gather_arrays(arrays, plan, sizes, collective_id):
    fit = [aligned(a.shape[p[1]], a, p[1]) for a, p in zip(arrays, plan)]
    if not all(fit):
        taken = [(a, p) for a, p, ok in zip(arrays, plan, fit) if ok]
        made = iter(gather_arrays([a for a, _ in taken], tuple(p for _, p in taken), sizes, collective_id))
        return [
            next(made) if ok else lax.all_gather(a, p[0], axis=p[1], tiled=True)
            for a, p, ok in zip(arrays, plan, fit)
        ]

    def full(array, axis, dim):
        return tuple(n * sizes[axis] if i == dim else n for i, n in enumerate(array.shape))

    slots = sum(sizes[axis] for axis, _, _ in plan)
    used = {axis: sizes[axis] for axis in sizes if any(a == axis for a, _, _ in plan)}
    return pl.pallas_call(
        functools.partial(gather_kernel, plan, used),
        out_shape=[jax.ShapeDtypeStruct(full(a, p[0], p[1]), a.dtype) for a, p in zip(arrays, plan)],
        in_specs=[pl.BlockSpec(memory_space=pl.ANY)] * len(arrays),
        out_specs=[pl.BlockSpec(memory_space=pl.ANY)] * len(arrays),
        scratch_shapes=[pltpu.VMEM(a.shape, a.dtype) for a in arrays]
        + [
            pltpu.SemaphoreType.DMA((3 * slots,)),
            pltpu.SemaphoreType.DMA((slots,)),
            pltpu.SemaphoreType.DMA((len(arrays), 2)),
        ],
        compiler_params=pltpu.CompilerParams(
            collective_id=collective_id, has_side_effects=True, vmem_limit_bytes=VMEM_BYTES
        ),
    )(*arrays)


def add_into(acc, other, shape):
    lead = shape[:-2]
    rows, cols = shape[-2:]
    block = 32
    while rows % block:
        block //= 2
    outer = 1
    for n in lead:
        outer *= n
    for index in itertools.product(*[range(n) for n in lead]):
        def step(r, carry, index=index):
            at = index + (pl.ds(pl.multiple_of(r * block, block), block), slice(None))
            acc[at] = (acc[at].astype(F32) + other[at].astype(F32)).astype(acc.dtype)
            return carry
        lax.fori_loop(0, rows // block, step, 0)


def fold_kernel(plan, sizes, order, *refs):
    count = len(plan)
    ins, outs = refs[:count], refs[count : 2 * count]
    across, along, stage = (refs[(2 + j) * count : (3 + j) * count] for j in range(3))
    x_send, x_recv, z_send, z_recv, load_sem, out_sem = refs[5 * count :]
    greet(sizes)
    xbase, zbase, sbase = [0], [0], [0]
    for axis, dim in plan:
        half = sizes[axis] // 2
        xbase.append(xbase[-1] + half)
        zbase.append(zbase[-1] + half + 1)
        sbase.append(sbase[-1] + 2 * half)

    def where(i):
        axis = plan[i][0]
        me = lax.axis_index(axis)
        return me, sizes[axis] // 2, me % 2, me // 2

    def size(i):
        axis, dim = plan[i]
        return ins[i].shape[dim] // sizes[axis]

    def exchange(i, place):
        me, half, side, _ = where(i)
        return pltpu.make_async_remote_copy(
            src_ref=part(ins[i], plan[i][1], place * 2 + 1 - side, size(i)),
            dst_ref=across[i].at[place],
            send_sem=x_send.at[xbase[i] + place],
            recv_sem=x_recv.at[xbase[i] + place],
            device_id={plan[i][0]: me + 1 - 2 * side},
            device_id_type=MESH,
        )

    def hop(i, owner, turn, dist, number):
        me, half, side, place = where(i)
        slot = half if (turn < 0 and dist == 1) else owner
        return pltpu.make_async_remote_copy(
            src_ref=across[i].at[owner],
            dst_ref=along[i].at[slot],
            send_sem=z_send.at[sbase[i] + number],
            recv_sem=z_recv.at[zbase[i] + slot],
            device_id={plan[i][0]: me + 2 * turn},
            device_id_type=MESH,
        )

    def landed(i, slot):
        me, half, side, place = where(i)
        pltpu.make_async_remote_copy(
            src_ref=along[i].at[slot], dst_ref=along[i].at[slot], send_sem=z_send.at[0],
            recv_sem=z_recv.at[zbase[i] + slot], device_id={plan[i][0]: me}, device_id_type=MESH,
        ).wait_recv()

    tasks = []
    for i, own in order:
        axis, dim = plan[i]
        half = sizes[axis] // 2
        if own:
            tasks.append((i, 0, 0))
        else:
            tasks += [(i, d, turn) for d in range(half - 1, 0, -1) for turn in (1, -1)]

    def valid(task):
        i, d, turn = task
        me, half, side, place = where(i)
        return None if d == 0 else (place + d < half if turn > 0 else place >= d)

    def guard(cond, fn):
        if cond is None:
            fn()
        else:
            pl.when(cond)(fn)

    parity = {}
    slots = []
    for task in tasks:
        parity[task[0]] = parity.get(task[0], -1) + 1
        slots.append(parity[task[0]] % 2)

    def load(n):
        i, d, turn = tasks[n]
        me, half, side, place = where(i)
        owner = place + turn * d
        return pltpu.make_async_copy(
            part(ins[i], plan[i][1], owner * 2 + side, size(i)), stage[i].at[slots[n]], load_sem.at[i, slots[n]]
        )

    guard(valid(tasks[0]), lambda: load(0).start())
    pushed = set()
    for i, own in order:
        if i in pushed:
            continue
        pushed.add(i)
        me, half, side, place = where(i)
        for d in range(half - 1, 0, -1):
            for turn in (1, -1):
                owner = place + turn * d
                pl.when(owner < half if turn > 0 else owner >= 0)(lambda i=i, owner=owner: exchange(i, owner).start())
        exchange(i, place).start()
    for n, task in enumerate(tasks):
        i, d, turn = task
        me, half, side, place = where(i)
        owner = place + turn * d
        shape = stage[i].shape[1:]
        if n + 1 < len(tasks):
            guard(valid(tasks[n + 1]), lambda n=n: load(n + 1).start())

        def work(n=n, i=i, d=d, turn=turn, owner=owner, shape=shape, half=half, place=place):
            exchange(i, owner).wait_recv()
            load(n).wait()
            add_into(across[i].at[owner], stage[i].at[slots[n]], shape)
            if d == 0:
                if half > 1:
                    for cond, slot in ((place > 0, place), (place < half - 1, half)):
                        @pl.when(cond)
                        def _(slot=slot):
                            landed(i, slot)
                            add_into(across[i].at[owner], along[i].at[slot], shape)
                pltpu.make_async_copy(across[i].at[owner], outs[i], out_sem.at[i]).start()
            else:
                @pl.when(place > 0 if turn > 0 else place < half - 1)
                def _():
                    landed(i, owner)
                    add_into(across[i].at[owner], along[i].at[owner], shape)
                hop(i, owner, turn, d, 2 * (d - 1) + (turn > 0)).start()

        guard(valid(task), work)
    for i, d, turn in tasks:
        me, half, side, place = where(i)
        owner = place + turn * d
        if d:
            guard(valid((i, d, turn)), lambda i=i, owner=owner, turn=turn, d=d: hop(i, owner, turn, d, 2 * (d - 1) + (turn > 0)).wait_send())
    for i in range(count):
        me, half, side, place = where(i)
        for p in range(half):
            exchange(i, p).wait_send()
        pltpu.make_async_copy(across[i].at[place], outs[i], out_sem.at[i]).wait()


def fold_arrays(arrays, plan, sizes, order, collective_id):
    fit = [aligned(a.shape[p[1]] // sizes[p[0]], a, p[1]) for a, p in zip(arrays, plan)]
    if not all(fit):
        taken = [i for i, ok in enumerate(fit) if ok]
        kept = tuple((taken.index(i), own) for i, own in order if fit[i])
        made = iter(
            fold_arrays([arrays[i] for i in taken], tuple(plan[i] for i in taken), sizes, kept, collective_id)
        )
        return [
            next(made) if ok else lax.psum_scatter(a, p[0], scatter_dimension=p[1], tiled=True)
            for a, p, ok in zip(arrays, plan, fit)
        ]

    used = {axis: sizes[axis] for axis in sizes if any(a == axis for a, _ in plan)}
    half = [sizes[axis] // 2 for axis, _ in plan]
    piece = [
        tuple(n // sizes[axis] if j == dim else n for j, n in enumerate(a.shape))
        for a, (axis, dim) in zip(arrays, plan)
    ]
    kinds = [a.dtype for a in arrays]
    dma = pltpu.SemaphoreType.DMA
    return pl.pallas_call(
        functools.partial(fold_kernel, plan, used, order),
        out_shape=[jax.ShapeDtypeStruct(p, k) for p, k in zip(piece, kinds)],
        in_specs=[pl.BlockSpec(memory_space=pl.ANY)] * len(arrays),
        out_specs=[pl.BlockSpec(memory_space=pl.ANY)] * len(arrays),
        scratch_shapes=[pltpu.VMEM((h,) + p, k) for h, p, k in zip(half, piece, kinds)]
        + [pltpu.VMEM((h + 1,) + p, k) for h, p, k in zip(half, piece, kinds)]
        + [pltpu.VMEM((2,) + p, k) for p, k in zip(piece, kinds)]
        + [
            dma((sum(half),)),
            dma((sum(half),)),
            dma((2 * sum(half),)),
            dma((sum(half) + len(half),)),
            dma((len(half), 2)),
            dma((len(half),)),
        ],
        compiler_params=pltpu.CompilerParams(
            collective_id=collective_id, has_side_effects=True, vmem_limit_bytes=67043328
        ),
    )(*arrays)


def dot(spec, left, right):
    return jnp.einsum(spec, left, right, preferred_element_type=F32)


def rotate(tensor, cosine, sine):
    half = tensor.shape[-1] // 2
    first, second = tensor[..., :half], tensor[..., half:]
    return jnp.concatenate([first * cosine - second * sine, first * sine + second * cosine], axis=-1)


def norm_back(grad_normed, source, inv_scale, gain):
    unit = source * inv_scale
    grad_unit = grad_normed * gain
    grad_source = inv_scale * (grad_unit - unit * jnp.mean(grad_unit * unit, axis=-1, keepdims=True))
    return grad_source, jnp.sum(grad_normed * unit, axis=0)


def swish_back(gate, up, grad_act):
    sig = jax.nn.sigmoid(gate)
    grad_gate = grad_act * up * sig * (1.0 + gate * (1.0 - sig))
    grad_up = grad_act * gate * sig
    return jnp.stack([grad_gate, grad_up]).astype(BF16)


def body(
    tokens, cotangent, segments, routes, gate_weight, gain_attn, w_qkv, b_qkv, w_out,
    gain_ffn, w_sgu, w_sd, shared_gate, w_egu, w_ed,
):
    micro, span, width = tokens.shape
    shards = lax.axis_size("shard")
    experts = lax.axis_size("expert") * w_egu.shape[0]
    own = w_egu.shape[0]
    count = micro * span
    length = span * shards
    heads = b_qkv.shape[1]
    score_scale = HD ** (-0.5)

    vectors = jnp.stack([gain_attn, gain_ffn, shared_gate])
    vectors = lax.all_gather(vectors, ("expert", "shard"), axis=1, tiled=True)
    bias = lax.all_gather(b_qkv, "expert", axis=2, tiled=True)
    sizes = {"expert": lax.axis_size("expert"), "shard": shards}
    low_rows = tokens.reshape(count, width)
    grad_low = cotangent.reshape(count, width)
    source_rows, grad_low_rows, egu, ed, qkv, sgu, sd, out = gather_arrays(
        (low_rows, grad_low, w_egu, w_ed, w_qkv, w_sgu, w_sd, w_out),
        (
            ("shard", 0, False),
            ("shard", 0, False),
            ("shard", 2, False),
            ("shard", 1, False),
            ("expert", 1, False),
            ("expert", 1, False),
            ("expert", 1, True),
            ("expert", 1, False),
        ),
        sizes,
        0,
    )

    gain_one, gain_two, gate_vec = (vectors[i].astype(F32) for i in range(3))
    source = low_rows.astype(F32)
    grad_out = grad_low.astype(F32)
    chosen = (routes.reshape(count, -1)[:, :, None] == jnp.arange(experts)).astype(F32)
    gates = jnp.sum(chosen * gate_weight.reshape(count, -1)[:, :, None], axis=1)
    gates = gates.T.reshape(-1, own, count)
    gates = lax.all_to_all(gates, "expert", split_axis=0, concat_axis=0, tiled=True)
    gates = gates.transpose(1, 0, 2).reshape(own, -1)
    grad_all = lax.all_gather(grad_low, "expert", axis=0, tiled=True)

    scale_one = lax.rsqrt(jnp.mean(source * source, axis=-1, keepdims=True) + EPSILON)
    rows_one = source_rows.astype(F32)
    rows_scale = lax.rsqrt(jnp.mean(rows_one * rows_one, axis=-1, keepdims=True) + EPSILON)
    rows_one = (rows_one * rows_scale * gain_one).astype(BF16)
    projected = dot("ld,ide->ile", rows_one, qkv) + bias.reshape(3, 1, -1).astype(F32)

    place = jnp.arange(length).astype(F32)
    frequency = ROPE_BASE ** (-jnp.arange(HD // 2).astype(F32) * 2.0 / HD)
    angles = place[:, None] * frequency[None, :]
    cosine, sine = jnp.cos(angles), jnp.sin(angles)

    def to_heads(rows):
        grid = rows.reshape(shards, micro, span, heads, HD).transpose(1, 3, 0, 2, 4)
        return grid.reshape(micro, heads, length, HD)

    def to_rows(grid):
        grid = grid.reshape(micro, heads, shards, span, HD).transpose(2, 0, 3, 1, 4)
        return grid.reshape(shards * count, heads * HD)

    queries = rotate(to_heads(projected[0]), cosine, sine).astype(BF16)
    keys = rotate(to_heads(projected[1]), cosine, sine).astype(BF16)
    values = to_heads(projected[2]).astype(BF16)
    labels = segments[:, 0]
    index = jnp.arange(length)
    allowed = (labels[:, :, None] == labels[:, None, :]) & (index[:, None] >= index[None, :])
    allowed = allowed[:, None]
    scores = jnp.where(allowed, dot("mhqd,mhkd->mhqk", queries, keys) * score_scale, -1e30)
    peak = jnp.max(scores, axis=-1, keepdims=True)
    expo = jnp.exp(scores - peak)
    total = jnp.sum(expo, axis=-1, keepdims=True)
    exact = expo / total
    probs = exact.astype(BF16)
    context = to_rows(dot("mhqk,mhkd->mhqd", probs, values).astype(BF16))
    attended = dot("le,ed->ld", context, out).astype(BF16)
    (attended,) = fold_arrays((attended,), (("shard", 0),), sizes, ((0, False), (0, True)), 1)
    hidden = source + attended.astype(F32)

    scale_two = lax.rsqrt(jnp.mean(hidden * hidden, axis=-1, keepdims=True) + EPSILON)
    normed_two = (hidden * scale_two * gain_two).astype(BF16)
    (rows_two,) = gather_arrays((normed_two,), (("shard", 0, False),), sizes, 2)
    routed = lax.all_gather(normed_two, "expert", axis=0, tiled=True)
    shared_in = dot("ld,idf->ilf", rows_two, sgu)
    shared_act = (jax.nn.silu(shared_in[0]) * shared_in[1]).astype(BF16)
    shared_part = dot("lf,fd->ld", shared_act, sd).astype(BF16)
    normed_float = normed_two.astype(F32)
    opening = jax.nn.sigmoid(jnp.sum(normed_float * gate_vec, axis=-1))
    opening_rows = jax.nn.sigmoid(jnp.sum(rows_two.astype(F32) * gate_vec, axis=-1))

    grad_shared_rows = (opening_rows[:, None] * grad_low_rows.astype(F32)).astype(BF16)
    grad_shared_act = dot("ld,fd->lf", grad_shared_rows, sd)
    grad_sd = dot("lf,ld->fd", shared_act, grad_shared_rows).astype(BF16)
    grad_shared_in = swish_back(shared_in[0], shared_in[1], grad_shared_act)
    grad_sgu = dot("ld,ilf->idf", rows_two, grad_shared_in).astype(BF16)
    grad_from_shared = dot("ilf,idf->ld", grad_shared_in, sgu).astype(BF16)
    routed, grad_sd, grad_sgu, grad_from_shared, shared_part = lax.optimization_barrier(
        (routed, grad_sd, grad_sgu, grad_from_shared, shared_part)
    )

    expert_in = dot("rd,jidf->ijrf", routed, egu)
    expert_act = (jax.nn.silu(expert_in[0]) * expert_in[1]).astype(BF16)
    expert_out = dot("jrf,jfd->jrd", expert_act, ed).astype(BF16).astype(F32)
    blend = jnp.sum(gates[:, :, None] * expert_out, axis=0).astype(BF16)
    blend = lax.psum_scatter(blend, "expert", scatter_dimension=0, tiled=True).astype(F32)
    grad_all_float = grad_all.astype(F32)
    inner = jnp.sum(expert_out * grad_all_float, axis=-1)
    inner = inner.reshape(own, -1, count).transpose(1, 0, 2)
    inner = lax.all_to_all(inner, "expert", split_axis=0, concat_axis=0, tiled=True)
    inner = inner.reshape(experts, count)
    grad_gate = jnp.sum(chosen * inner.T[:, None, :], axis=-1)

    grad_expert = (gates[:, :, None] * grad_all_float).astype(BF16)
    grad_expert_act = dot("jrd,jfd->jrf", grad_expert, ed)
    grad_ed = dot("jrf,jrd->jfd", expert_act, grad_expert).astype(BF16)
    grad_expert_in = swish_back(expert_in[0], expert_in[1], grad_expert_act)
    grad_routed = dot("ijrf,jidf->rd", grad_expert_in, egu).astype(BF16)
    grad_egu = dot("rd,ijrf->jidf", routed, grad_expert_in).astype(BF16)
    grad_routed, grad_egu, grad_ed = lax.optimization_barrier((grad_routed, grad_egu, grad_ed))
    grad_from_experts, shared_sum, grad_from_shared = fold_arrays(
        (grad_routed, shared_part, grad_from_shared),
        (("expert", 0), ("shard", 0), ("shard", 0)),
        sizes,
        ((1, False), (2, False), (0, False), (1, True), (2, True), (0, True)),
        3,
    )
    shared_sum = shared_sum.astype(F32)
    mixed = hidden + opening[:, None] * shared_sum + blend

    grad_opening = jnp.sum(grad_out * shared_sum, axis=-1)
    grad_logit = grad_opening * opening * (1.0 - opening)
    grad_gate_vec = jnp.sum(grad_logit[:, None] * normed_float, axis=0)
    grad_normed_two = grad_from_experts.astype(F32) + grad_from_shared.astype(F32) + grad_logit[:, None] * gate_vec
    grad_hidden, grad_gain_two = norm_back(grad_normed_two, hidden, scale_two, gain_two)
    grad_hidden = grad_out + grad_hidden

    (grad_rows,) = gather_arrays((grad_hidden.astype(BF16),), (("shard", 0, False),), sizes, 4)
    grad_context = to_heads(dot("ld,ed->le", grad_rows, out).astype(BF16))
    grad_out_w = dot("le,ld->ed", context, grad_rows).astype(BF16)
    grad_probs = dot("mhqd,mhkd->mhqk", grad_context, values)
    delta = jnp.sum(exact * grad_probs, axis=-1, keepdims=True)
    grad_scores = (exact * (grad_probs - delta)).astype(BF16)
    grad_values = dot("mhqk,mhqd->mhkd", probs, grad_context)
    grad_queries = dot("mhqk,mhkd->mhqd", grad_scores, keys) * score_scale
    grad_keys = dot("mhqk,mhqd->mhkd", grad_scores, queries) * score_scale
    grad_projected = jnp.stack(
        [
            to_rows(rotate(grad_queries, cosine, -sine)),
            to_rows(rotate(grad_keys, cosine, -sine)),
            to_rows(grad_values),
        ]
    ).astype(BF16)
    grad_bias = jnp.sum(grad_projected.astype(F32), axis=1).reshape(3, heads, HD)
    grad_qkv = dot("ld,ile->ide", rows_one, grad_projected).astype(BF16)
    grad_normed_one = dot("ile,ide->ld", grad_projected, qkv).astype(BF16)
    (grad_normed_one,) = fold_arrays((grad_normed_one,), (("shard", 0),), sizes, ((0, False), (0, True)), 5)
    grad_normed_one, grad_qkv, grad_out_w = lax.optimization_barrier((grad_normed_one, grad_qkv, grad_out_w))
    grad_normed_one = grad_normed_one.astype(F32)
    grad_source, grad_gain_one = norm_back(grad_normed_one, source, scale_one, gain_one)
    grad_tokens = grad_hidden + grad_source

    folded = fold_arrays(
        (grad_egu, grad_ed, grad_sgu, grad_qkv, grad_sd, grad_out_w),
        (("shard", 2), ("shard", 1), ("expert", 1), ("expert", 1), ("expert", 1), ("expert", 1)),
        sizes,
        tuple((i, own) for i, own in (
            (0, False), (1, False), (2, False), (2, True), (3, False), (3, True),
            (0, True), (1, True), (4, False), (4, True), (5, False), (5, True),
        )),
        6,
    )
    summed_egu, summed_ed, summed_sgu, summed_qkv, summed_sd, summed_out = (x.astype(F32) for x in folded)
    summed_bias = lax.psum_scatter(grad_bias, "expert", scatter_dimension=2, tiled=True)
    gains = jnp.stack([grad_gain_one, grad_gain_two, grad_gate_vec])
    gains = lax.psum_scatter(gains, ("expert", "shard"), scatter_dimension=1, tiled=True)
    shape = tokens.shape
    return (
        mixed.reshape(shape),
        grad_tokens.reshape(shape),
        grad_gate.reshape(routes.shape),
        gains[0],
        summed_qkv,
        summed_bias,
        summed_out,
        gains[1],
        summed_sgu,
        summed_sd,
        gains[2],
        summed_egu,
        summed_ed,
    )


def solution(mesh):
    both = ("expert", "shard")
    rows = P(None, both, None)
    parameters = (
        P(None, "expert", "shard"),
        P(None, "shard", "expert"),
        P("shard", "expert"),
        P(both),
        P(None, "expert", "shard"),
        P("shard", "expert"),
        P(both),
        P("expert", None, "shard", None),
        P("expert", "shard", None),
    )
    return jax.shard_map(
        body,
        mesh=mesh,
        in_specs=(rows, rows, P(None, "expert", None), rows, rows, P(both)) + parameters,
        out_specs=(rows, rows, rows, P(both)) + parameters,
        check_vma=False,
    )
```
